32 devices in a mesh: dp: 8 (over y, x, core), expert: 4 (over z).
Axes of the slice: x: 2, y: 2, z: 4, core: 2. Of those that a mesh axis runs over, the one named last changes fastest.
Arguments:
- tokens: bfloat16 [4096, 4096], P(('dp', 'expert')), may hold values from -6 to 6
- probs: bfloat16 [4096, 1], P(('dp', 'expert')), may hold values from 0.19921875 to 1
- routes: int32 [4096, 1], P(('dp', 'expert')), may hold values from 0 to 3; in each aligned block of 128 rows (0 to 127, 128 to 255, ...) at most 34 rows name the same one
- w_gate: bfloat16 [4, 4096, 1024], P('expert', 'dp'), may hold values from -0.09375 to 0.09375
- w_up: bfloat16 [4, 4096, 1024], P('expert', 'dp'), may hold values from -0.09375 to 0.09375
- w_down: bfloat16 [4, 1024, 4096], P('expert', None, 'dp'), may hold values from -0.1875 to 0.1875
- cotangent: bfloat16 [4096, 4096], P(('dp', 'expert')), may hold values from -6 to 6
Outputs:
- mixed: bfloat16 [4096, 4096], P(('dp', 'expert'))
- input_grad: bfloat16 [4096, 4096], P(('dp', 'expert'))
- grad_gate: bfloat16 [4, 4096, 1024], P('expert', 'dp')
- grad_up: bfloat16 [4, 4096, 1024], P('expert', 'dp')
- grad_down: bfloat16 [4, 1024, 4096], P('expert', None, 'dp')
The draws below stay inside these ranges and needn't reach their ends.
Inputs may be any that keep to these rules, and one draw needn't show every extreme that they name: `routes`: each row names exactly one expert. Among the 128 rows of one device (aligned blocks), no expert is named more than 34 times, a bound that some block reaches.
All inputs are finite; a program needn't handle non-finite values.
Results may differ from the reference program's by a relative error of at most 0.025.
Values may be sent and summed in bfloat16 or wider, within the bound.
A program may use at most 128 MiB of HBM per device.

```python
import math
import jax
import jax.numpy as jnp
import numpy as np
from jax import lax

D = 4096
FF = 1024
TOP = 1
TOK_DEV = 128
EXPERTS = 4
CAP = 34
TOKENS = 4096
N_DP = 8
N_EXPERT = 4


def block_levels(stream_key, extent, pieces, least, largest):
    gain = 1.0
    for axis_at, shards_of in pieces:
        heights = jax.random.uniform(jax.random.fold_in(jax.random.fold_in(stream_key, 6), axis_at), (shards_of,), jnp.float32, least / len(pieces), largest / len(pieces))
        gain = gain * jnp.repeat(jnp.exp(heights), extent[axis_at] // shards_of).reshape((-1,) + (1,) * (len(extent) - 1 - axis_at))
    return gain


def shared_out(own_key, own, number, rows, count, top, most, lean):
    ranking = jax.random.permutation(own_key, count)
    packed, usual = shares(count, rows * top, most, lean, True), shares(count, rows * top, most, lean, False)
    places = jnp.arange(count)

    def named(sizes, rotation):
        used = int((sizes > 0).sum())
        fixed = max(1, used // 4)
        shifted = fixed + (places - fixed + rotation * (used - fixed)) % max(1, count - fixed)
        return jnp.zeros((count,), jnp.int32).at[ranking[jnp.where(places < fixed, places, shifted)]].set(jnp.asarray(sizes, jnp.int32))

    sizes = jnp.where(number % 4 == 0, named(packed, number // 4), named(usual, number - number // 4 - 1))
    mixed = jax.random.permutation(jax.random.fold_in(own, 3), count)
    giver, receiver = mixed[0:count // 2 * 2:2], mixed[1:count // 2 * 2:2]
    room = jnp.minimum(sizes[giver] - 1, most - sizes[receiver]) // 2
    room = jnp.where((giver == ranking[0]) | (receiver == ranking[0]) | (sizes[receiver] == 0), 0, jnp.maximum(room, 0))
    shifted = jax.random.randint(jax.random.fold_in(own, 4), (count // 2,), 0, 1 << 20) % (room + 1)
    sizes = sizes.at[giver].add(-shifted).at[receiver].add(shifted)
    labels = jnp.searchsorted(jnp.cumsum(sizes), jnp.arange(rows * top), side="right").astype(jnp.int32)
    listing = labels.reshape(top, rows).T
    listing = listing[jax.random.permutation(jax.random.fold_in(own, 1), rows)]
    rotation = jax.random.randint(jax.random.fold_in(own, 2), (rows, 1), 0, top)
    return jnp.take_along_axis(listing, (jnp.arange(top)[None, :] + rotation) % top, axis=1)


def shares(number_of, total, reach, lean, full):
    loads = [(1 << 20) // math.isqrt(grade ** lean) + 1 for grade in range(1, number_of + 1)]
    largest = reach if full else min(reach, max(-(-total // number_of), total * loads[0] // sum(loads)))
    least = 1 if total - largest >= number_of - 1 else 0
    holding, rest = [largest] + [least] * (number_of - 1), total - largest - least * (number_of - 1)
    while rest > 0:
        free = [i for i in range(1, number_of) if holding[i] < largest] or [i for i in range(1, number_of) if holding[i] < reach]
        whole, left = sum([loads[i] for i in free]), rest
        for i in free:
            extra = min(reach - holding[i], max(1, left * loads[i] // whole), rest)
            holding[i] = holding[i] + extra
            rest = rest - extra
    return np.array(holding)


def centred(rng, shape, scale, bound, shards=(), held_as=jnp.bfloat16):
    loudness = block_levels(rng, shape, shards, -0.22, 0.18) if shards else 1.0
    values = jax.random.normal(rng, shape, jnp.float32) * scale * loudness
    return jnp.minimum(jnp.maximum(values, -bound), bound).astype(held_as)


def setup_inputs(seed: int = 0) -> dict:
    seeds = jax.random.split(jax.random.key(seed), 8)
    tokens = centred(seeds[0], (TOKENS, D), 1.0, 6.0, ((0, 32),))
    probs = jnp.clip(jnp.exp(math.log(1.0) - 1.6133518 * jax.random.uniform(seeds[1], (TOKENS, TOP), jnp.float32) ** block_levels(seeds[1], (TOKENS, TOP), ((0, 32),), -0.2, 0.2)), 0.19921875, 1.0).astype(jnp.bfloat16)
    routes_keys = jax.random.split(jax.random.fold_in(seeds[2], 1), TOKENS // TOK_DEV)
    routes_turns = jax.random.permutation(jax.random.fold_in(seeds[2], 3), TOKENS // TOK_DEV)
    routes = jax.vmap(lambda own, number: shared_out(jax.random.fold_in(seeds[2], 2), own, number, TOK_DEV, EXPERTS, TOP, CAP, 2))(routes_keys, routes_turns).reshape((TOKENS, TOP))
    w_gate = centred(seeds[3], (EXPERTS, D, FF), D ** -0.5, 0.09375, ((0, 4), (1, 8)))
    w_up = centred(seeds[4], (EXPERTS, D, FF), D ** -0.5, 0.09375, ((0, 4), (1, 8)))
    w_down = centred(seeds[5], (EXPERTS, FF, D), FF ** -0.5, 0.1875, ((0, 4), (2, 8)))
    cotangent = centred(seeds[6], (TOKENS, D), 1.0, 6.0, ((0, 32),))
    return dict(tokens=tokens, probs=probs, routes=routes, w_gate=w_gate, w_up=w_up, w_down=w_down, cotangent=cotangent)


def split_sum(left, right):
    parts = jnp.einsum("rnk,nkf->nrf", left.astype(jnp.float32), right.astype(jnp.float32),
                       precision=lax.Precision.HIGHEST)
    rounded = lax.optimization_barrier(parts.astype(jnp.bfloat16))
    return jnp.sum(rounded.astype(jnp.float32), axis=0)


def reference(tokens, probs, routes, w_gate, w_up, w_down, cotangent):
    flat_route = routes.reshape(-1)
    flat_prob = probs.reshape(-1)
    most = N_DP * N_EXPERT * CAP
    slices = D // N_DP

    def one_expert(carry, expert):
        mixed_sum, input_sum = carry
        hit = flat_route == expert
        pick = jnp.nonzero(hit, size=most, fill_value=0)[0].astype(jnp.int32)
        valid = jnp.arange(most, dtype=jnp.int32) < jnp.sum(hit.astype(jnp.int32))
        keep = valid.astype(jnp.float32)
        owner = (pick // TOP).astype(jnp.int32)
        rows = tokens[owner] * valid[:, None].astype(jnp.bfloat16)
        weight = flat_prob[pick].astype(jnp.float32) * keep
        gate_w = lax.dynamic_index_in_dim(w_gate, expert, 0, keepdims=False)
        up_w = lax.dynamic_index_in_dim(w_up, expert, 0, keepdims=False)
        down_w = lax.dynamic_index_in_dim(w_down, expert, 0, keepdims=False)
        split_rows = rows.reshape(most, N_DP, slices)
        gate_pre = split_sum(split_rows, gate_w.reshape(N_DP, slices, FF))
        up_value = split_sum(split_rows, up_w.reshape(N_DP, slices, FF))
        sig = jax.nn.sigmoid(gate_pre)
        act = (gate_pre * sig * up_value).astype(jnp.bfloat16)
        result = jnp.dot(act, down_w, preferred_element_type=jnp.float32).astype(jnp.bfloat16)
        mixed_sum = mixed_sum.at[owner].add(result.astype(jnp.float32) * weight[:, None])
        dout = (cotangent[owner].astype(jnp.float32) * weight[:, None]).astype(jnp.bfloat16)
        grad_down = jnp.dot(act.T, dout, preferred_element_type=jnp.float32).astype(jnp.bfloat16)
        down_split = jnp.transpose(down_w.reshape(FF, N_DP, slices), (1, 2, 0))
        dact = split_sum(dout.reshape(most, N_DP, slices), down_split)
        dgate = (dact * up_value * sig * (1.0 + gate_pre * (1.0 - sig))).astype(jnp.bfloat16)
        dup = (dact * gate_pre * sig).astype(jnp.bfloat16)
        grad_gate = jnp.dot(rows.T, dgate, preferred_element_type=jnp.float32).astype(jnp.bfloat16)
        grad_up = jnp.dot(rows.T, dup, preferred_element_type=jnp.float32).astype(jnp.bfloat16)
        slot_grad = (jnp.dot(dgate, gate_w.T, preferred_element_type=jnp.float32)
                     + jnp.dot(dup, up_w.T, preferred_element_type=jnp.float32)).astype(jnp.bfloat16)
        input_sum = input_sum.at[owner].add(slot_grad.astype(jnp.float32) * keep[:, None])
        return (mixed_sum, input_sum), (grad_gate, grad_up, grad_down)

    start = (jnp.zeros((TOKENS, D), jnp.float32), jnp.zeros((TOKENS, D), jnp.float32))
    (mixed_sum, input_sum), grads = lax.scan(one_expert, start, jnp.arange(EXPERTS, dtype=jnp.int32))
    return (mixed_sum.astype(jnp.bfloat16), input_sum.astype(jnp.bfloat16), grads[0], grads[1], grads[2])
```

```python
import functools

import jax
import jax.numpy as jnp
from jax import lax
from jax.experimental import pallas as pl
from jax.experimental.pallas import tpu as pltpu
from jax.sharding import PartitionSpec as P

BF = jnp.bfloat16
F32 = jnp.float32


def nn(a, b):
    return lax.dot_general(a, b, (((1,), (0,)), ((), ())), preferred_element_type=F32)


def nt(a, b):
    return lax.dot_general(a, b, (((1,), (1,)), ((), ())), preferred_element_type=F32)


def tn(a, b):
    return lax.dot_general(a, b, (((0,), (0,)), ((), ())), preferred_element_type=F32)


def layer_kernel(
    n, e_n, cap,
    tok, dys, tgt, wg, wu, wd,
    res_o, ig_o, gg_o, gu_o, gd_o,
    tga, table, xa, da, xs, ds_, xr, dr, xp, dp, pwg, pwu, pwd,
    gs, gr, hs, hr, pre, upv, act, dga, dua, rs, rr, ss, sr, un, un2, x_t,
    sem_dp, sem_pw, sem_ex, sem_q,
):
    m = lax.axis_index("dp")
    z = lax.axis_index("expert")
    q_n = n // 2
    q = m // 2
    c = lax.rem(m, 2)
    pm = m + 1 - 2 * c
    slots = n * cap
    t_rows, w = tok.shape[0], tok.shape[1] // n
    ff = wg.shape[1]
    fh = ff // 2
    b = fh // q_n

    def rows(k):
        return pl.ds(pl.multiple_of(k * slots, 16), slots)

    def toks(k):
        return pl.ds(pl.multiple_of(k * t_rows, 128), t_rows)

    def cols(k):
        return pl.ds(pl.multiple_of(k * w, 128), w)

    my_half = pl.ds(pl.multiple_of(c * fh, 128), fh)
    other_half = pl.ds(pl.multiple_of((1 - c) * fh, 128), fh)

    def block(qq):
        return pl.ds(pl.multiple_of(c * fh + qq * b, 128), b)

    def copy(src, dst, send, recv, dp_at, ex_at):
        return pltpu.make_async_remote_copy(
            src_ref=src, dst_ref=dst, send_sem=send, recv_sem=recv,
            device_id=(dp_at, ex_at), device_id_type=pl.DeviceIdType.MESH,
        )

    def dp_pair(no, src, dst):
        def out(i):
            return copy(src(i), dst(m), sem_dp.at[2 * no, i], sem_dp.at[2 * no + 1, m], i, z)

        def got(i):
            return copy(src(i), dst(i), sem_dp.at[2 * no, i], sem_dp.at[2 * no + 1, i], i, z)

        return out, got

    def ex_pair(no, src, dst):
        def out(i):
            return copy(src.at[rows(i)], dst.at[rows(z)], sem_ex.at[2 * no, i], sem_ex.at[2 * no + 1, z], m, i)

        def got(i):
            return copy(src.at[rows(i)], dst.at[rows(i)], sem_ex.at[2 * no, i], sem_ex.at[2 * no + 1, i], m, i)

        return out, got

    def pass_pair(no, src, dst):
        def out(k):
            return copy(src(k), src(k) if dst is None else dst(k), sem_ex.at[2 * no, k], sem_ex.at[2 * no + 1, k], pm, z)

        return out

    def q_pair(no, src, dst):
        def out(k, i):
            return copy(src(k, i), dst(k, q), sem_q.at[2 * no, k, i], sem_q.at[2 * no + 1, k, q], 2 * i + c, z)

        def got(k, i):
            return copy(src(k, i), dst(k, i), sem_q.at[2 * no, k, i], sem_q.at[2 * no + 1, k, i], 2 * i + c, z)

        return out, got

    tg_out, tg_got = dp_pair(0, lambda i: tgt, lambda i: tga.at[i])
    xa_out, xa_got = dp_pair(1, lambda i: tok.at[:, cols(i)], lambda i: xa.at[toks(i)])
    da_out, da_got = dp_pair(2, lambda i: dys.at[:, cols(i)], lambda i: da.at[toks(i)])
    re_out, re_got = dp_pair(3, lambda i: un.at[toks(i)], lambda i: res_o.at[:, cols(i)])
    ig_out, ig_got = dp_pair(4, lambda i: un2.at[toks(i)], lambda i: ig_o.at[:, cols(i)])
    xe_out, xe_got = ex_pair(0, xs, xr)
    de_out, de_got = ex_pair(1, ds_, dr)
    rb_out, rb_got = ex_pair(2, rs, rr)
    sb_out, sb_got = ex_pair(3, ss, sr)
    xf = pass_pair(4, lambda k: xr.at[rows(k)], lambda k: xp.at[rows(k)])
    df = pass_pair(5, lambda k: dr.at[rows(k)], lambda k: dp.at[rows(k)])

    def half_pass(no, ref):
        send, recv = sem_ex.at[2 * no], sem_ex.at[2 * no + 1]

        def out(k):
            part = ref.at[rows(k), my_half]
            return copy(part, part, send.at[k], recv.at[k], pm, z)

        def got(k):
            part = ref.at[rows(k), other_half]
            return copy(part, part, send.at[k], recv.at[k], pm, z)

        return out, got

    af_out, af_got = half_pass(6, act)
    ef_out, ef_got = half_pass(7, dga)
    uf_out, uf_got = half_pass(8, dua)
    g_out, g_got = q_pair(0, lambda k, i: gs.at[k, i], lambda k, i: gr.at[k, i])
    h_out, h_got = q_pair(1, lambda k, i: hs.at[k, i], lambda k, i: hr.at[k, i])

    def share_pair(no, ref):
        def out(k, i):
            part = ref.at[rows(k), block(q)]
            return copy(part, part, sem_q.at[2 * no, k, i], sem_q.at[2 * no + 1, k, q], 2 * i + c, z)

        def got(k, i):
            part = ref.at[rows(k), block(i)]
            return copy(part, part, sem_q.at[2 * no, k, i], sem_q.at[2 * no + 1, k, i], 2 * i + c, z)

        return out, got

    a_out, a_got = share_pair(2, act)
    e_out, e_got = share_pair(3, dga)
    u_out, u_got = share_pair(4, dua)
    pw = [
        copy(wg.at[:, other_half], pwg, sem_pw.at[0, 0], sem_pw.at[1, 0], pm, z),
        copy(wu.at[:, other_half], pwu, sem_pw.at[0, 1], sem_pw.at[1, 1], pm, z),
        copy(wd.at[other_half], pwd, sem_pw.at[0, 2], sem_pw.at[1, 2], pm, z),
    ]

    def loop(lo, hi, body):
        def step(i, carry):
            body(i)
            return carry

        lax.fori_loop(lo, hi, step, 0)

    def dp_others(body):
        loop(1, n, lambda d: body(lax.rem(m + d, n)))

    def ex_others(body):
        loop(1, e_n, lambda d: body(lax.rem(z + d, e_n)))

    def q_others(body):
        for d in range(1, q_n):
            body(lax.rem(q + d, q_n))

    def chunks(body):
        loop(0, e_n, lambda d: body(d, lax.rem(z + e_n - d, e_n)))

    barrier = pltpu.get_barrier_semaphore()
    dp_others(lambda i: pl.semaphore_signal(
        barrier, inc=1, device_id=(i, z), device_id_type=pl.DeviceIdType.MESH))
    ex_others(lambda i: pl.semaphore_signal(
        barrier, inc=1, device_id=(m, i), device_id_type=pl.DeviceIdType.MESH))
    pl.semaphore_wait(barrier, n - 1 + e_n - 1)

    dp_others(lambda i: tg_out(i).start())
    dp_others(lambda i: xa_out(i).start())
    for one in pw:
        one.start()
    dp_others(lambda i: da_out(i).start())
    tga[m] = tgt[...]
    xa[toks(m), :] = tok[:, cols(m)]
    da[toks(m), :] = dys[:, cols(m)]
    dp_others(lambda i: tg_got(i).wait_recv())
    for i in range(n):
        names = tga[i][0:1, :]
        place = lax.broadcasted_iota(jnp.int32, (e_n * slots, t_rows), 0)
        table[:, i * t_rows:(i + 1) * t_rows] = jnp.where(place == names, 1.0, 0.0).astype(BF)

    def slot_out(src, buf, own, out):
        def one(d):
            e = lax.rem(z + d, e_n)
            buf[rows(e), :] = nn(table[rows(e), :], src[...]).astype(BF)
            out(e).start()

        loop(1, e_n, one)
        own[rows(z), :] = nn(table[rows(z), :], src[...]).astype(BF)

    dp_others(lambda i: xa_got(i).wait_recv())
    slot_out(xa, xs, xr, xe_out)
    dp_others(lambda i: da_got(i).wait_recv())
    slot_out(da, ds_, dr, de_out)
    for one in pw:
        one.wait_recv()

    def gate_up(d, k):
        @pl.when(d > 0)
        def _():
            xe_got(k).wait_recv()

        xf(k).start()
        xf(k).wait_recv()
        for at, own_w, other_w in ((0, wg, pwg), (1, wu, pwu)):
            part = nn(xr[rows(k), :], own_w[:, my_half]) + nn(xp[rows(k), :], other_w[...])
            part = part.astype(BF)
            for i in range(q_n):
                gs[k, i, :, at * b:(at + 1) * b] = part[:, i * b:(i + 1) * b]
        q_others(lambda i: g_out(k, i).start())

    chunks(gate_up)

    def activate(d, k):
        total = gs[k, q].astype(F32)
        for dd in range(1, q_n):
            i = lax.rem(q + dd, q_n)
            g_got(k, i).wait_recv()
            total = total + gr[k, i].astype(F32)
        gate, up = total[:, :b], total[:, b:]
        pre[rows(k), :] = gate
        upv[rows(k), :] = up
        act[rows(k), block(q)] = (gate * jax.nn.sigmoid(gate) * up).astype(BF)
        q_others(lambda i: a_out(k, i).start())

    chunks(activate)

    def down(d, k):
        q_others(lambda i: a_got(k, i).wait_recv())
        af_out(k).start()

        @pl.when(d > 0)
        def _():
            de_got(k).wait_recv()

        df(k).start()
        df(k).wait_recv()
        part = nt(dr[rows(k), :], wd[my_half, :]) + nt(dp[rows(k), :], pwd[...])
        part = part.astype(BF)
        for i in range(q_n):
            hs[k, i] = part[:, i * b:(i + 1) * b]
        q_others(lambda i: h_out(k, i).start())
        af_got(k).wait_recv()
        result = nn(act[rows(k), :], wd[...]).astype(BF)

        @pl.when(d == 0)
        def _():
            rr[rows(k), :] = result

        @pl.when(d > 0)
        def _():
            rs[rows(k), :] = result
            rb_out(k).start()

    chunks(down)

    def act_grad(d, k):
        total = hs[k, q].astype(F32)
        for dd in range(1, q_n):
            i = lax.rem(q + dd, q_n)
            h_got(k, i).wait_recv()
            total = total + hr[k, i].astype(F32)
        gate, up = pre[rows(k), :], upv[rows(k), :]
        sig = jax.nn.sigmoid(gate)
        dga[rows(k), block(q)] = (total * up * sig * (1.0 + gate * (1.0 - sig))).astype(BF)
        dua[rows(k), block(q)] = (total * gate * sig).astype(BF)
        q_others(lambda i: e_out(k, i).start())
        q_others(lambda i: u_out(k, i).start())

    chunks(act_grad)

    x_t[...] = xr[...].T
    tile = 2 * b

    def down_grad(j):
        at = pl.ds(pl.multiple_of(j * tile, 128), tile)
        gd_o[at, :] = tn(act[:, at], dr[...]).astype(BF)

    loop(0, ff // tile, down_grad)

    def handed(d, k):
        q_others(lambda i: e_got(k, i).wait_recv())
        ef_out(k).start()
        q_others(lambda i: u_got(k, i).wait_recv())
        uf_out(k).start()

    chunks(handed)

    def input_grad(d, k):
        ef_got(k).wait_recv()
        uf_got(k).wait_recv()
        value = (nt(dga[rows(k), :], wg[...]) + nt(dua[rows(k), :], wu[...])).astype(BF)

        @pl.when(d == 0)
        def _():
            sr[rows(k), :] = value

        @pl.when(d > 0)
        def _():
            ss[rows(k), :] = value
            sb_out(k).start()

    chunks(input_grad)

    def give_back(src, buf, out):
        def one(d):
            i = lax.rem(m + d, n)
            buf[toks(i), :] = tn(table[:, toks(i)], src[...]).astype(BF)
            out(i).start()

        loop(1, n, one)
        buf[toks(m), :] = tn(table[:, toks(m)], src[...]).astype(BF)

    ex_others(lambda i: rb_got(i).wait_recv())
    give_back(rr, un, re_out)
    res_o[:, cols(m)] = un[toks(m), :]

    def weight_grad(j):
        at = pl.ds(pl.multiple_of(j * tile, 128), tile)
        gg_o[:, at] = nn(x_t[...], dga[:, at]).astype(BF)
        gu_o[:, at] = nn(x_t[...], dua[:, at]).astype(BF)

    loop(0, ff // tile, weight_grad)
    ex_others(lambda i: sb_got(i).wait_recv())
    give_back(sr, un2, ig_out)
    ig_o[:, cols(m)] = un2[toks(m), :]

    def dp_end(i):
        re_got(i).wait_recv()
        ig_got(i).wait_recv()
        for out in (tg_out, xa_out, da_out, re_out, ig_out):
            out(i).wait_send()

    dp_others(dp_end)

    def ex_end(i):
        for out in (xe_out, de_out, rb_out, sb_out):
            out(i).wait_send()

    ex_others(ex_end)
    for one in pw:
        one.wait_send()

    def chunk_end(k):
        for out in (xf, df, af_out, ef_out, uf_out):
            out(k).wait_send()
        for out in (g_out, h_out, a_out, e_out, u_out):
            q_others(lambda i: out(k, i).wait_send())

    loop(0, e_n, chunk_end)


def fused_layer(tokens, probs, routes, w_gate, w_up, w_down, cotangent, n, e_n, cap):
    t_rows, width = tokens.shape
    w = width // n
    ff = w_gate.shape[2]
    slots, fh, q_n = n * cap, ff // 2, n // 2
    b = fh // q_n
    r = e_n * slots
    weight = probs.astype(F32)
    dys = (cotangent.astype(F32) * weight).astype(BF)
    flat = routes.reshape(-1)
    hits = (flat[:, None] == jnp.arange(e_n, dtype=jnp.int32)[None, :]).astype(jnp.int32)
    before = jnp.cumsum(hits, axis=0) - hits
    place = jnp.sum(before * hits, axis=1)
    target = flat * slots + lax.axis_index("dp").astype(jnp.int32) * cap + place
    tgt = jnp.broadcast_to(target[None, :], (8, t_rows))
    vm = pl.BlockSpec(memory_space=pltpu.VMEM)

    def v(*shape, dtype=BF):
        return pltpu.VMEM(shape, dtype)

    scratch = [
        v(n, 8, t_rows, dtype=jnp.int32), v(r, n * t_rows),
        v(n * t_rows, w), v(n * t_rows, w),
        v(r, w), v(r, w), v(r, w), v(r, w), v(r, w), v(r, w),
        v(w, fh), v(w, fh), v(fh, w),
        v(e_n, q_n, slots, 2 * b), v(e_n, q_n, slots, 2 * b),
        v(e_n, q_n, slots, b), v(e_n, q_n, slots, b),
        v(r, b, dtype=F32), v(r, b, dtype=F32),
        v(r, ff), v(r, ff), v(r, ff),
        v(r, w), v(r, w), v(r, w), v(r, w),
        v(n * t_rows, w), v(n * t_rows, w), v(w, r),
        pltpu.SemaphoreType.DMA((10, n)),
        pltpu.SemaphoreType.DMA((2, 3)),
        pltpu.SemaphoreType.DMA((18, e_n)),
        pltpu.SemaphoreType.DMA((10, e_n, q_n)),
    ]
    result, input_grad, gg, gu, gd = pl.pallas_call(
        functools.partial(layer_kernel, n, e_n, cap),
        out_shape=(
            jax.ShapeDtypeStruct((t_rows, width), BF),
            jax.ShapeDtypeStruct((t_rows, width), BF),
            jax.ShapeDtypeStruct((w, ff), BF),
            jax.ShapeDtypeStruct((w, ff), BF),
            jax.ShapeDtypeStruct((ff, w), BF),
        ),
        in_specs=[vm] * 6,
        out_specs=(vm,) * 5,
        scratch_shapes=scratch,
        compiler_params=pltpu.CompilerParams(
            collective_id=0, has_side_effects=True, vmem_limit_bytes=62 * 1024 * 1024
        ),
    )(tokens, dys, tgt, w_gate[0], w_up[0], w_down[0])
    mixed = (result.astype(F32) * weight).astype(BF)
    return mixed, input_grad, gg[None], gu[None], gd[None]


def slot_table(routes, experts_all, capacity):
    flat = routes.reshape(-1)
    hits = (flat[:, None] == jnp.arange(experts_all, dtype=jnp.int32)[None, :]).astype(jnp.int32)
    before = jnp.cumsum(hits, axis=0) - hits
    place = jnp.sum(before * hits, axis=1)
    target = flat * capacity + place
    table = jnp.arange(experts_all * capacity, dtype=jnp.int32)[:, None] == target[None, :]
    return table.astype(jnp.bfloat16)


def spread_rows(table, values, slices):
    shaped = values.reshape(values.shape[0], slices, values.shape[1] // slices)
    return jnp.einsum("st,tnk->nsk", table, shaped, preferred_element_type=jnp.float32).astype(
        jnp.bfloat16
    )


def to_rows(received, local_count):
    sources, slots, width = received.shape
    shaped = received.reshape(sources, local_count, slots // local_count, width)
    shaped = jnp.swapaxes(shaped, 1, 2)
    return shaped.reshape(sources * (slots // local_count), local_count, width)


def to_sources(rowwise, capacity):
    total, local_count, width = rowwise.shape
    shaped = rowwise.reshape(total // capacity, capacity, local_count, width)
    shaped = jnp.swapaxes(shaped, 1, 2)
    return shaped.reshape(total // capacity, local_count * capacity, width)


def collect(table, back, tok_rows, top):
    picked = jnp.einsum("st,nsk->tnk", table, back, preferred_element_type=jnp.float32)
    return picked.reshape(tok_rows, top, -1)


def per_device(tokens, probs, routes, w_gate, w_up, w_down, cotangent):
    local_count = w_gate.shape[0]
    n_dp = lax.axis_size("dp")
    n_exp = lax.axis_size("expert")
    experts_all = local_count * n_exp
    tok_rows, width = tokens.shape
    top = routes.shape[1]
    capacity = max(2, 17 * tok_rows * top // (16 * experts_all))
    ff = w_gate.shape[2]
    if (
        local_count == 1 and top == 1 and n_dp % 2 == 0 and ff % (n_dp * 128) == 0
        and tok_rows % 128 == 0 and width % (n_dp * 128) == 0 and (n_dp * capacity) % 16 == 0
    ):
        return fused_layer(
            tokens, probs, routes, w_gate, w_up, w_down, cotangent, n_dp, n_exp, capacity
        )
    blocks = n_dp * n_exp
    slot_width = width // n_dp
    table = slot_table(routes, experts_all, capacity)
    x_send = spread_rows(table, jnp.repeat(tokens, top, axis=0), n_dp)
    x_send = x_send.reshape(blocks, local_count * capacity, slot_width)
    weight = probs.astype(jnp.float32)
    scaled = (jnp.repeat(cotangent, top, axis=0).astype(jnp.float32) * weight).astype(jnp.bfloat16)
    x_got = lax.all_to_all(x_send, ("dp", "expert"), split_axis=0, concat_axis=0, tiled=True)
    rows = to_rows(x_got, local_count)
    part = rows
    gate = jnp.einsum("red,edf->ref", part, w_gate, preferred_element_type=jnp.float32)
    upper = jnp.einsum("red,edf->ref", part, w_up, preferred_element_type=jnp.float32)
    summed = lax.psum_scatter(
        jnp.stack([gate, upper], axis=2).astype(jnp.bfloat16), "dp", scatter_dimension=0, tiled=True
    ).astype(jnp.float32)
    gate_pre = summed[:, :, 0]
    up_value = summed[:, :, 1]
    sig = jax.nn.sigmoid(gate_pre)
    act = (gate_pre * sig * up_value).astype(jnp.bfloat16)
    act_all = lax.all_gather(act, "dp", axis=0, tiled=True)
    result = jnp.einsum("ref,efd->red", act_all, w_down, preferred_element_type=jnp.float32).astype(
        jnp.bfloat16
    )
    outgoing = to_sources(result, capacity)
    back = lax.all_to_all(outgoing, ("dp", "expert"), split_axis=0, concat_axis=0, tiled=True)
    back = back.reshape(n_dp, experts_all * capacity, slot_width)
    picked = collect(table, back, tok_rows, top)
    mixed = jnp.sum(picked * weight[..., None], axis=1).astype(jnp.bfloat16)
    dy_send = spread_rows(table, scaled, n_dp).reshape(blocks, local_count * capacity, slot_width)
    dy_got = lax.all_to_all(dy_send, ("dp", "expert"), split_axis=0, concat_axis=0, tiled=True)
    dout = to_rows(dy_got, local_count)
    grad_down = jnp.einsum("ref,red->efd", act_all, dout, preferred_element_type=jnp.float32)
    part = dout
    dact = lax.psum_scatter(
        jnp.einsum("red,efd->ref", part, w_down, preferred_element_type=jnp.float32).astype(
            jnp.bfloat16
        ),
        "dp",
        scatter_dimension=0,
        tiled=True,
    ).astype(jnp.float32)
    dgate = (dact * up_value * sig * (1.0 + gate_pre * (1.0 - sig))).astype(jnp.bfloat16)
    dup = (dact * gate_pre * sig).astype(jnp.bfloat16)
    dgate_all, dup_all = (
        lax.all_gather(dgate, "dp", axis=0, tiled=True),
        lax.all_gather(dup, "dp", axis=0, tiled=True),
    )
    grad_gate = jnp.einsum("red,ref->edf", rows, dgate_all, preferred_element_type=jnp.float32)
    grad_up = jnp.einsum("red,ref->edf", rows, dup_all, preferred_element_type=jnp.float32)
    slot_grad = jnp.einsum(
        "ref,edf->red", dgate_all, w_gate, preferred_element_type=jnp.float32
    ) + jnp.einsum("ref,edf->red", dup_all, w_up, preferred_element_type=jnp.float32)
    slot_grad = slot_grad.astype(jnp.bfloat16)
    returned = lax.all_to_all(
        to_sources(slot_grad, capacity), ("dp", "expert"), split_axis=0, concat_axis=0, tiled=True
    )
    returned = returned.reshape(n_dp, experts_all * capacity, slot_width)
    input_grad = jnp.sum(collect(table, returned, tok_rows, top), axis=1).astype(jnp.bfloat16)
    return (
        mixed,
        input_grad,
        grad_gate.astype(jnp.bfloat16),
        grad_up.astype(jnp.bfloat16),
        grad_down.astype(jnp.bfloat16),
    )


def solution(mesh):
    return jax.shard_map(
        per_device,
        mesh=mesh,
        in_specs=(
            P(("dp", "expert"), None),
            P(("dp", "expert"), None),
            P(("dp", "expert"), None),
            P("expert", "dp", None),
            P("expert", "dp", None),
            P("expert", None, "dp"),
            P(("dp", "expert"), None),
        ),
        out_specs=(
            P(("dp", "expert"), None),
            P(("dp", "expert"), None),
            P("expert", "dp", None),
            P("expert", "dp", None),
            P("expert", None, "dp"),
        ),
        check_vma=False,
    )
```

```python
import functools

import jax
import jax.numpy as jnp
from jax import lax
from jax.experimental import pallas as pl
from jax.experimental.pallas import tpu as pltpu
from jax.sharding import PartitionSpec as P

BF = jnp.bfloat16
F32 = jnp.float32


def nn(a, b):
    return lax.dot_general(a, b, (((1,), (0,)), ((), ())), preferred_element_type=F32)


def nt(a, b):
    return lax.dot_general(a, b, (((1,), (1,)), ((), ())), preferred_element_type=F32)


def tn(a, b):
    return lax.dot_general(a, b, (((0,), (0,)), ((), ())), preferred_element_type=F32)


def layer_kernel(
    n, e_n, cap,
    tok, cot, tgt, wt, wg, wu, wd,
    res_o, ig_o, gg_o, gu_o, gd_o,
    tga, table, xa, da, xs, ds_, xr, dr, xp, dp, pwg, pwu, pwd,
    gs, gr, hs, hr, pre, upv, act, dga, dua, rs, rr, ss, sr, un, un2, x_t, dys,
    sem_dp, sem_pw, sem_ex, sem_q,
):
    m = lax.axis_index("dp")
    z = lax.axis_index("expert")
    q_n = n // 2
    q = m // 2
    c = lax.rem(m, 2)
    pm = m + 1 - 2 * c
    slots = n * cap
    t_rows, w = tok.shape[0], tok.shape[1] // n
    ff = wg.shape[1]
    fh = ff // 2
    b = fh // q_n

    def rows(k):
        return pl.ds(pl.multiple_of(k * slots, 16), slots)

    def toks(k):
        return pl.ds(pl.multiple_of(k * t_rows, 128), t_rows)

    def cols(k):
        return pl.ds(pl.multiple_of(k * w, 128), w)

    my_half = pl.ds(pl.multiple_of(c * fh, 128), fh)
    other_half = pl.ds(pl.multiple_of((1 - c) * fh, 128), fh)

    def block(qq):
        return pl.ds(pl.multiple_of(c * fh + qq * b, 128), b)

    def copy(src, dst, send, recv, dp_at, ex_at):
        return pltpu.make_async_remote_copy(
            src_ref=src, dst_ref=dst, send_sem=send, recv_sem=recv,
            device_id=(dp_at, ex_at), device_id_type=pl.DeviceIdType.MESH,
        )

    def dp_pair(no, src, dst):
        def out(i):
            return copy(src(i), dst(m), sem_dp.at[2 * no, i], sem_dp.at[2 * no + 1, m], i, z)

        def got(i):
            return copy(src(i), dst(i), sem_dp.at[2 * no, i], sem_dp.at[2 * no + 1, i], i, z)

        return out, got

    def ex_pair(no, src, dst):
        def out(i):
            return copy(src.at[rows(i)], dst.at[rows(z)], sem_ex.at[2 * no, i], sem_ex.at[2 * no + 1, z], m, i)

        def got(i):
            return copy(src.at[rows(i)], dst.at[rows(i)], sem_ex.at[2 * no, i], sem_ex.at[2 * no + 1, i], m, i)

        return out, got

    def pass_pair(no, src, dst):
        def out(k):
            return copy(src(k), src(k) if dst is None else dst(k), sem_ex.at[2 * no, k], sem_ex.at[2 * no + 1, k], pm, z)

        return out

    def q_pair(no, src, dst):
        def out(k, i):
            return copy(src(k, i), dst(k, q), sem_q.at[2 * no, k, i], sem_q.at[2 * no + 1, k, q], 2 * i + c, z)

        def got(k, i):
            return copy(src(k, i), dst(k, i), sem_q.at[2 * no, k, i], sem_q.at[2 * no + 1, k, i], 2 * i + c, z)

        return out, got

    tg_out, tg_got = dp_pair(0, lambda i: tgt, lambda i: tga.at[i])
    xa_out, xa_got = dp_pair(1, lambda i: tok.at[:, cols(i)], lambda i: xa.at[toks(i)])
    da_out, da_got = dp_pair(2, lambda i: dys.at[:, cols(i)], lambda i: da.at[toks(i)])
    re_out, re_got = dp_pair(3, lambda i: un.at[toks(i)], lambda i: res_o.at[:, cols(i)])
    ig_out, ig_got = dp_pair(4, lambda i: un2.at[toks(i)], lambda i: ig_o.at[:, cols(i)])
    xe_out, xe_got = ex_pair(0, xs, xr)
    de_out, de_got = ex_pair(1, ds_, dr)
    rb_out, rb_got = ex_pair(2, rs, rr)
    sb_out, sb_got = ex_pair(3, ss, sr)
    xf = pass_pair(4, lambda k: xr.at[rows(k)], lambda k: xp.at[rows(k)])
    df = pass_pair(5, lambda k: dr.at[rows(k)], lambda k: dp.at[rows(k)])

    def half_pass(no, ref):
        send, recv = sem_ex.at[2 * no], sem_ex.at[2 * no + 1]

        def out(k):
            part = ref.at[rows(k), my_half]
            return copy(part, part, send.at[k], recv.at[k], pm, z)

        def got(k):
            part = ref.at[rows(k), other_half]
            return copy(part, part, send.at[k], recv.at[k], pm, z)

        return out, got

    af_out, af_got = half_pass(6, act)
    ef_out, ef_got = half_pass(7, dga)
    uf_out, uf_got = half_pass(8, dua)
    g_out, g_got = q_pair(0, lambda k, i: gs.at[k, i], lambda k, i: gr.at[k, i])
    h_out, h_got = q_pair(1, lambda k, i: hs.at[k, i], lambda k, i: hr.at[k, i])

    def share_pair(no, ref):
        def out(k, i):
            part = ref.at[rows(k), block(q)]
            return copy(part, part, sem_q.at[2 * no, k, i], sem_q.at[2 * no + 1, k, q], 2 * i + c, z)

        def got(k, i):
            part = ref.at[rows(k), block(i)]
            return copy(part, part, sem_q.at[2 * no, k, i], sem_q.at[2 * no + 1, k, i], 2 * i + c, z)

        return out, got

    a_out, a_got = share_pair(2, act)
    e_out, e_got = share_pair(3, dga)
    u_out, u_got = share_pair(4, dua)
    pw = [
        copy(wg.at[:, other_half], pwg, sem_pw.at[0, 0], sem_pw.at[1, 0], pm, z),
        copy(wu.at[:, other_half], pwu, sem_pw.at[0, 1], sem_pw.at[1, 1], pm, z),
        copy(wd.at[other_half], pwd, sem_pw.at[0, 2], sem_pw.at[1, 2], pm, z),
    ]

    def loop(lo, hi, body):
        def step(i, carry):
            body(i)
            return carry

        lax.fori_loop(lo, hi, step, 0)

    def partner(at, d, size):
        if size & (size - 1):
            return lax.rem(at + d, size)
        other, step = at, 1
        while step < size:
            if d & step:
                other = other + step - 2 * step * lax.rem(at // step, 2)
            step *= 2
        return other

    def dp_others(body):
        for d in range(1, n):
            body(partner(m, d, n))

    def ex_others(body):
        loop(1, e_n, lambda d: body(lax.rem(z + d, e_n)))

    def q_others(body):
        for d in range(1, q_n):
            body(partner(q, d, q_n))

    def chunks(body):
        loop(0, e_n, lambda d: body(d, lax.rem(z + e_n - d, e_n)))

    def far_first(body):
        loop(1, e_n + 1, lambda d: body(d, lax.rem(z + 2 * e_n - d, e_n)))

    def ahead(first, then):
        def step(d):
            @pl.when(d <= e_n)
            def _():
                first(lax.rem(z + 2 * e_n - d, e_n))

            @pl.when(d > 1)
            def _():
                then(d - 1, lax.rem(z + 2 * e_n - (d - 1), e_n))

        loop(1, e_n + 2, step)

    barrier = pltpu.get_barrier_semaphore()
    dp_others(lambda i: pl.semaphore_signal(
        barrier, inc=1, device_id=(i, z), device_id_type=pl.DeviceIdType.MESH))
    ex_others(lambda i: pl.semaphore_signal(
        barrier, inc=1, device_id=(m, i), device_id_type=pl.DeviceIdType.MESH))
    pl.semaphore_wait(barrier, n - 1 + e_n - 1)

    dp_others(lambda i: tg_out(i).start())
    dp_others(lambda i: xa_out(i).start())
    for one in pw:
        one.start()
    wide = tok.shape[1] // 8
    for i in range(8):
        at = slice(i * wide, (i + 1) * wide)
        dys[:, at] = (cot[:, at].astype(F32) * wt[...]).astype(BF)
    dp_others(lambda i: da_out(i).start())
    tga[m] = tgt[...]
    xa[toks(m), :] = tok[:, cols(m)]
    da[toks(m), :] = dys[:, cols(m)]
    dp_others(lambda i: tg_got(i).wait_recv())
    for i in range(n):
        names = tga[i][0:1, :]
        place = lax.broadcasted_iota(jnp.int32, (e_n * slots, t_rows), 0)
        table[:, i * t_rows:(i + 1) * t_rows] = jnp.where(place == names, 1.0, 0.0).astype(BF)

    def slot_out(src, buf, own, out):
        def one(d):
            e = lax.rem(z + d, e_n)
            buf[rows(e), :] = nn(table[rows(e), :], src[...]).astype(BF)
            out(e).start()

        loop(1, e_n, one)
        own[rows(z), :] = nn(table[rows(z), :], src[...]).astype(BF)

    dp_others(lambda i: xa_got(i).wait_recv())
    slot_out(xa, xs, xr, xe_out)
    dp_others(lambda i: da_got(i).wait_recv())
    slot_out(da, ds_, dr, de_out)
    for one in pw:
        one.wait_recv()

    def gate_up(d, k):
        @pl.when(d > 0)
        def _():
            xe_got(k).wait_recv()

        xf(k).start()
        xf(k).wait_recv()
        for at, own_w, other_w in ((0, wg, pwg), (1, wu, pwu)):
            part = nn(xr[rows(k), :], own_w[:, my_half]) + nn(xp[rows(k), :], other_w[...])
            part = part.astype(BF)
            for i in range(q_n):
                gs[k, i, :, at * b:(at + 1) * b] = part[:, i * b:(i + 1) * b]
        q_others(lambda i: g_out(k, i).start())

    chunks(gate_up)

    def activate(d, k):
        total = gs[k, q].astype(F32)
        for dd in range(1, q_n):
            i = partner(q, dd, q_n)
            g_got(k, i).wait_recv()
            total = total + gr[k, i].astype(F32)
        gate, up = total[:, :b], total[:, b:]
        pre[rows(k), :] = gate
        upv[rows(k), :] = up
        act[rows(k), block(q)] = (gate * jax.nn.sigmoid(gate) * up).astype(BF)
        q_others(lambda i: a_out(k, i).start())

    far_first(activate)

    def down(d, k):
        @pl.when(d > 0)
        def _():
            de_got(k).wait_recv()

        df(k).start()
        df(k).wait_recv()
        part = nt(dr[rows(k), :], wd[my_half, :]) + nt(dp[rows(k), :], pwd[...])
        part = part.astype(BF)
        for i in range(q_n):
            hs[k, i] = part[:, i * b:(i + 1) * b]
        q_others(lambda i: h_out(k, i).start())

    chunks(down)

    def act_pass(k):
        q_others(lambda i: a_got(k, i).wait_recv())
        af_out(k).start()

    def result_rows(d, k):
        af_got(k).wait_recv()
        result = nn(act[rows(k), :], wd[...]).astype(BF)

        @pl.when(d == e_n)
        def _():
            rr[rows(k), :] = result

        @pl.when(d < e_n)
        def _():
            rs[rows(k), :] = result
            rb_out(k).start()

    ahead(act_pass, result_rows)

    def act_grad(d, k):
        total = hs[k, q].astype(F32)
        for dd in range(1, q_n):
            i = partner(q, dd, q_n)
            h_got(k, i).wait_recv()
            total = total + hr[k, i].astype(F32)
        gate, up = pre[rows(k), :], upv[rows(k), :]
        sig = jax.nn.sigmoid(gate)
        dga[rows(k), block(q)] = (total * up * sig * (1.0 + gate * (1.0 - sig))).astype(BF)
        dua[rows(k), block(q)] = (total * gate * sig).astype(BF)
        q_others(lambda i: e_out(k, i).start())
        q_others(lambda i: u_out(k, i).start())

    far_first(act_grad)

    def handed(k):
        q_others(lambda i: e_got(k, i).wait_recv())
        ef_out(k).start()
        q_others(lambda i: u_got(k, i).wait_recv())
        uf_out(k).start()

    def input_grad(d, k):
        ef_got(k).wait_recv()
        uf_got(k).wait_recv()
        value = (nt(dga[rows(k), :], wg[...]) + nt(dua[rows(k), :], wu[...])).astype(BF)

        @pl.when(d == e_n)
        def _():
            sr[rows(k), :] = value

        @pl.when(d < e_n)
        def _():
            ss[rows(k), :] = value
            sb_out(k).start()

    ahead(handed, input_grad)

    x_t[...] = xr[...].T
    tile = 2 * b

    def down_grad(j):
        at = pl.ds(pl.multiple_of(j * tile, 128), tile)
        gd_o[at, :] = tn(act[:, at], dr[...]).astype(BF)

    loop(0, ff // tile, down_grad)

    def give_back(src, buf, out):
        def one(d):
            i = partner(m, d, n)
            buf[toks(i), :] = tn(table[:, toks(i)], src[...]).astype(BF)
            out(i).start()

        for d in range(1, n):
            one(d)
        buf[toks(m), :] = tn(table[:, toks(m)], src[...]).astype(BF)

    ex_others(lambda i: rb_got(i).wait_recv())
    give_back(rr, un, re_out)
    res_o[:, cols(m)] = un[toks(m), :]

    def weight_grad(j):
        at = pl.ds(pl.multiple_of(j * tile, 128), tile)
        gg_o[:, at] = nn(x_t[...], dga[:, at]).astype(BF)
        gu_o[:, at] = nn(x_t[...], dua[:, at]).astype(BF)

    loop(0, ff // tile, weight_grad)
    ex_others(lambda i: sb_got(i).wait_recv())
    give_back(sr, un2, ig_out)
    ig_o[:, cols(m)] = un2[toks(m), :]

    def dp_end(i):
        re_got(i).wait_recv()
        ig_got(i).wait_recv()
        for out in (tg_out, xa_out, da_out, re_out, ig_out):
            out(i).wait_send()

    dp_others(dp_end)

    def ex_end(i):
        for out in (xe_out, de_out, rb_out, sb_out):
            out(i).wait_send()

    ex_others(ex_end)
    for one in pw:
        one.wait_send()

    def chunk_end(k):
        for out in (xf, df, af_out, ef_out, uf_out):
            out(k).wait_send()
        for out in (g_out, h_out, a_out, e_out, u_out):
            q_others(lambda i: out(k, i).wait_send())

    loop(0, e_n, chunk_end)


def fused_layer(tokens, probs, routes, w_gate, w_up, w_down, cotangent, n, e_n, cap):
    t_rows, width = tokens.shape
    w = width // n
    ff = w_gate.shape[2]
    slots, fh, q_n = n * cap, ff // 2, n // 2
    b = fh // q_n
    r = e_n * slots
    weight = probs.astype(F32)
    flat = routes.reshape(-1)
    hits = (flat[:, None] == jnp.arange(e_n, dtype=jnp.int32)[None, :]).astype(jnp.int32)
    before = jnp.cumsum(hits, axis=0) - hits
    place = jnp.sum(before * hits, axis=1)
    target = flat * slots + lax.axis_index("dp").astype(jnp.int32) * cap + place
    tgt = jnp.broadcast_to(target[None, :], (8, t_rows))
    vm = pl.BlockSpec(memory_space=pltpu.VMEM)

    def v(*shape, dtype=BF):
        return pltpu.VMEM(shape, dtype)

    scratch = [
        v(n, 8, t_rows, dtype=jnp.int32), v(r, n * t_rows),
        v(n * t_rows, w), v(n * t_rows, w),
        v(r, w), v(r, w), v(r, w), v(r, w), v(r, w), v(r, w),
        v(w, fh), v(w, fh), v(fh, w),
        v(e_n, q_n, slots, 2 * b), v(e_n, q_n, slots, 2 * b),
        v(e_n, q_n, slots, b), v(e_n, q_n, slots, b),
        v(r, b, dtype=F32), v(r, b, dtype=F32),
        v(r, ff), v(r, ff), v(r, ff),
        v(r, w), v(r, w), v(r, w), v(r, w),
        v(n * t_rows, w), v(n * t_rows, w), v(w, r), v(t_rows, width),
        pltpu.SemaphoreType.DMA((10, n)),
        pltpu.SemaphoreType.DMA((2, 3)),
        pltpu.SemaphoreType.DMA((18, e_n)),
        pltpu.SemaphoreType.DMA((10, e_n, q_n)),
    ]
    result, input_grad, gg, gu, gd = pl.pallas_call(
        functools.partial(layer_kernel, n, e_n, cap),
        out_shape=(
            jax.ShapeDtypeStruct((t_rows, width), BF),
            jax.ShapeDtypeStruct((t_rows, width), BF),
            jax.ShapeDtypeStruct((w, ff), BF),
            jax.ShapeDtypeStruct((w, ff), BF),
            jax.ShapeDtypeStruct((ff, w), BF),
        ),
        in_specs=[vm] * 7,
        out_specs=(vm,) * 5,
        scratch_shapes=scratch,
        compiler_params=pltpu.CompilerParams(
            collective_id=0, has_side_effects=True, vmem_limit_bytes=62 * 1024 * 1024
        ),
    )(tokens, cotangent, tgt, weight, w_gate[0], w_up[0], w_down[0])
    mixed = (result.astype(F32) * weight).astype(BF)
    return mixed, input_grad, gg[None], gu[None], gd[None]


def slot_table(routes, experts_all, capacity):
    flat = routes.reshape(-1)
    hits = (flat[:, None] == jnp.arange(experts_all, dtype=jnp.int32)[None, :]).astype(jnp.int32)
    before = jnp.cumsum(hits, axis=0) - hits
    place = jnp.sum(before * hits, axis=1)
    target = flat * capacity + place
    table = jnp.arange(experts_all * capacity, dtype=jnp.int32)[:, None] == target[None, :]
    return table.astype(jnp.bfloat16)


def spread_rows(table, values, slices):
    shaped = values.reshape(values.shape[0], slices, values.shape[1] // slices)
    return jnp.einsum("st,tnk->nsk", table, shaped, preferred_element_type=jnp.float32).astype(
        jnp.bfloat16
    )


def to_rows(received, local_count):
    sources, slots, width = received.shape
    shaped = received.reshape(sources, local_count, slots // local_count, width)
    shaped = jnp.swapaxes(shaped, 1, 2)
    return shaped.reshape(sources * (slots // local_count), local_count, width)


def to_sources(rowwise, capacity):
    total, local_count, width = rowwise.shape
    shaped = rowwise.reshape(total // capacity, capacity, local_count, width)
    shaped = jnp.swapaxes(shaped, 1, 2)
    return shaped.reshape(total // capacity, local_count * capacity, width)


def collect(table, back, tok_rows, top):
    picked = jnp.einsum("st,nsk->tnk", table, back, preferred_element_type=jnp.float32)
    return picked.reshape(tok_rows, top, -1)


def per_device(tokens, probs, routes, w_gate, w_up, w_down, cotangent):
    local_count = w_gate.shape[0]
    n_dp = lax.axis_size("dp")
    n_exp = lax.axis_size("expert")
    experts_all = local_count * n_exp
    tok_rows, width = tokens.shape
    top = routes.shape[1]
    capacity = max(2, 17 * tok_rows * top // (16 * experts_all))
    ff = w_gate.shape[2]
    if (
        local_count == 1 and top == 1 and n_dp % 2 == 0 and ff % (n_dp * 128) == 0
        and tok_rows % 128 == 0 and width % (n_dp * 128) == 0 and (n_dp * capacity) % 16 == 0
    ):
        return fused_layer(
            tokens, probs, routes, w_gate, w_up, w_down, cotangent, n_dp, n_exp, capacity
        )
    blocks = n_dp * n_exp
    slot_width = width // n_dp
    table = slot_table(routes, experts_all, capacity)
    x_send = spread_rows(table, jnp.repeat(tokens, top, axis=0), n_dp)
    x_send = x_send.reshape(blocks, local_count * capacity, slot_width)
    weight = probs.astype(jnp.float32)
    scaled = (jnp.repeat(cotangent, top, axis=0).astype(jnp.float32) * weight).astype(jnp.bfloat16)
    x_got = lax.all_to_all(x_send, ("dp", "expert"), split_axis=0, concat_axis=0, tiled=True)
    rows = to_rows(x_got, local_count)
    part = rows
    gate = jnp.einsum("red,edf->ref", part, w_gate, preferred_element_type=jnp.float32)
    upper = jnp.einsum("red,edf->ref", part, w_up, preferred_element_type=jnp.float32)
    summed = lax.psum_scatter(
        jnp.stack([gate, upper], axis=2).astype(jnp.bfloat16), "dp", scatter_dimension=0, tiled=True
    ).astype(jnp.float32)
    gate_pre = summed[:, :, 0]
    up_value = summed[:, :, 1]
    sig = jax.nn.sigmoid(gate_pre)
    act = (gate_pre * sig * up_value).astype(jnp.bfloat16)
    act_all = lax.all_gather(act, "dp", axis=0, tiled=True)
    result = jnp.einsum("ref,efd->red", act_all, w_down, preferred_element_type=jnp.float32).astype(
        jnp.bfloat16
    )
    outgoing = to_sources(result, capacity)
    back = lax.all_to_all(outgoing, ("dp", "expert"), split_axis=0, concat_axis=0, tiled=True)
    back = back.reshape(n_dp, experts_all * capacity, slot_width)
    picked = collect(table, back, tok_rows, top)
    mixed = jnp.sum(picked * weight[..., None], axis=1).astype(jnp.bfloat16)
    dy_send = spread_rows(table, scaled, n_dp).reshape(blocks, local_count * capacity, slot_width)
    dy_got = lax.all_to_all(dy_send, ("dp", "expert"), split_axis=0, concat_axis=0, tiled=True)
    dout = to_rows(dy_got, local_count)
    grad_down = jnp.einsum("ref,red->efd", act_all, dout, preferred_element_type=jnp.float32)
    part = dout
    dact = lax.psum_scatter(
        jnp.einsum("red,efd->ref", part, w_down, preferred_element_type=jnp.float32).astype(
            jnp.bfloat16
        ),
        "dp",
        scatter_dimension=0,
        tiled=True,
    ).astype(jnp.float32)
    dgate = (dact * up_value * sig * (1.0 + gate_pre * (1.0 - sig))).astype(jnp.bfloat16)
    dup = (dact * gate_pre * sig).astype(jnp.bfloat16)
    dgate_all, dup_all = (
        lax.all_gather(dgate, "dp", axis=0, tiled=True),
        lax.all_gather(dup, "dp", axis=0, tiled=True),
    )
    grad_gate = jnp.einsum("red,ref->edf", rows, dgate_all, preferred_element_type=jnp.float32)
    grad_up = jnp.einsum("red,ref->edf", rows, dup_all, preferred_element_type=jnp.float32)
    slot_grad = jnp.einsum(
        "ref,edf->red", dgate_all, w_gate, preferred_element_type=jnp.float32
    ) + jnp.einsum("ref,edf->red", dup_all, w_up, preferred_element_type=jnp.float32)
    slot_grad = slot_grad.astype(jnp.bfloat16)
    returned = lax.all_to_all(
        to_sources(slot_grad, capacity), ("dp", "expert"), split_axis=0, concat_axis=0, tiled=True
    )
    returned = returned.reshape(n_dp, experts_all * capacity, slot_width)
    input_grad = jnp.sum(collect(table, returned, tok_rows, top), axis=1).astype(jnp.bfloat16)
    return (
        mixed,
        input_grad,
        grad_gate.astype(jnp.bfloat16),
        grad_up.astype(jnp.bfloat16),
        grad_down.astype(jnp.bfloat16),
    )


def solution(mesh):
    return jax.shard_map(
        per_device,
        mesh=mesh,
        in_specs=(
            P(("dp", "expert"), None),
            P(("dp", "expert"), None),
            P(("dp", "expert"), None),
            P("expert", "dp", None),
            P("expert", "dp", None),
            P("expert", None, "dp"),
            P(("dp", "expert"), None),
        ),
        out_specs=(
            P(("dp", "expert"), None),
            P(("dp", "expert"), None),
            P("expert", "dp", None),
            P("expert", "dp", None),
            P("expert", None, "dp"),
        ),
        check_vma=False,
    )
```

```python
import functools

import jax
import jax.numpy as jnp
from jax import lax
from jax.experimental import pallas as pl
from jax.experimental.pallas import tpu as pltpu
from jax.sharding import PartitionSpec as P

BF = jnp.bfloat16
F32 = jnp.float32


def nn(a, b):
    return lax.dot_general(a, b, (((1,), (0,)), ((), ())), preferred_element_type=F32)


def nt(a, b):
    return lax.dot_general(a, b, (((1,), (1,)), ((), ())), preferred_element_type=F32)


def tn(a, b):
    return lax.dot_general(a, b, (((0,), (0,)), ((), ())), preferred_element_type=F32)


def layer_kernel(
    n, e_n, cap,
    tok, cot, tgt, wt, wg_h, wu_h, wd_h,
    res_o, ig_o, gg_o, gu_o, gd_o,
    tga, table, xa, da, xs, ds_, xr, dr, xp, dp, pwg, pwu, pwd,
    gs, gr, hs, hr, pre, upv, act, dga, dua, rs, rr, ss, sr, un, un2, x_t, dys, wg, wu, wd,
    sem_own, sem_dp, sem_pw, sem_ex, sem_q,
):
    m = lax.axis_index("dp")
    z = lax.axis_index("expert")
    q_n = n // 2
    q = m // 2
    c = lax.rem(m, 2)
    pm = m + 1 - 2 * c
    slots = n * cap
    t_rows, w = tok.shape[0], tok.shape[1] // n
    ff = wg_h.shape[1]
    fh = ff // 2
    b = fh // q_n

    def rows(k):
        return pl.ds(pl.multiple_of(k * slots, 16), slots)

    def toks(k):
        return pl.ds(pl.multiple_of(k * t_rows, 128), t_rows)

    def cols(k):
        return pl.ds(pl.multiple_of(k * w, 128), w)

    my_half = pl.ds(pl.multiple_of(c * fh, 128), fh)
    other_half = pl.ds(pl.multiple_of((1 - c) * fh, 128), fh)

    def block(qq):
        return pl.ds(pl.multiple_of(c * fh + qq * b, 128), b)

    def copy(src, dst, send, recv, dp_at, ex_at):
        return pltpu.make_async_remote_copy(
            src_ref=src, dst_ref=dst, send_sem=send, recv_sem=recv,
            device_id=(dp_at, ex_at), device_id_type=pl.DeviceIdType.MESH,
        )

    def dp_pair(no, src, dst):
        def out(i):
            return copy(src(i), dst(m), sem_dp.at[2 * no, i], sem_dp.at[2 * no + 1, m], i, z)

        def got(i):
            return copy(src(i), dst(i), sem_dp.at[2 * no, i], sem_dp.at[2 * no + 1, i], i, z)

        return out, got

    def ex_pair(no, src, dst):
        def out(i):
            return copy(src.at[rows(i)], dst.at[rows(z)], sem_ex.at[2 * no, i], sem_ex.at[2 * no + 1, z], m, i)

        def got(i):
            return copy(src.at[rows(i)], dst.at[rows(i)], sem_ex.at[2 * no, i], sem_ex.at[2 * no + 1, i], m, i)

        return out, got

    def pass_pair(no, src, dst):
        def out(k):
            return copy(src(k), src(k) if dst is None else dst(k), sem_ex.at[2 * no, k], sem_ex.at[2 * no + 1, k], pm, z)

        return out

    def q_pair(no, src, dst):
        def out(k, i):
            return copy(src(k, i), dst(k, q), sem_q.at[2 * no, k, i], sem_q.at[2 * no + 1, k, q], 2 * i + c, z)

        def got(k, i):
            return copy(src(k, i), dst(k, i), sem_q.at[2 * no, k, i], sem_q.at[2 * no + 1, k, i], 2 * i + c, z)

        return out, got

    tg_out, tg_got = dp_pair(0, lambda i: tgt, lambda i: tga.at[i])
    xa_out, xa_got = dp_pair(1, lambda i: tok.at[:, cols(i)], lambda i: xa.at[toks(i)])
    da_out, da_got = dp_pair(2, lambda i: dys.at[:, cols(i)], lambda i: da.at[toks(i)])
    re_out, re_got = dp_pair(3, lambda i: un.at[toks(i)], lambda i: res_o.at[:, cols(i)])
    ig_out, ig_got = dp_pair(4, lambda i: un2.at[toks(i)], lambda i: ig_o.at[:, cols(i)])
    xe_out, xe_got = ex_pair(0, xs, xr)
    de_out, de_got = ex_pair(1, ds_, dr)
    rb_out, rb_got = ex_pair(2, rs, rr)
    sb_out, sb_got = ex_pair(3, ss, sr)
    xf = pass_pair(4, lambda k: xr.at[rows(k)], lambda k: xp.at[rows(k)])
    df = pass_pair(5, lambda k: dr.at[rows(k)], lambda k: dp.at[rows(k)])

    def half_pass(no, ref):
        send, recv = sem_ex.at[2 * no], sem_ex.at[2 * no + 1]

        def out(k):
            part = ref.at[rows(k), my_half]
            return copy(part, part, send.at[k], recv.at[k], pm, z)

        def got(k):
            part = ref.at[rows(k), other_half]
            return copy(part, part, send.at[k], recv.at[k], pm, z)

        return out, got

    af_out, af_got = half_pass(6, act)
    ef_out, ef_got = half_pass(7, dga)
    uf_out, uf_got = half_pass(8, dua)
    g_out, g_got = q_pair(0, lambda k, i: gs.at[k, i], lambda k, i: gr.at[k, i])
    h_out, h_got = q_pair(1, lambda k, i: hs.at[k, i], lambda k, i: hr.at[k, i])

    def share_pair(no, ref):
        def out(k, i):
            part = ref.at[rows(k), block(q)]
            return copy(part, part, sem_q.at[2 * no, k, i], sem_q.at[2 * no + 1, k, q], 2 * i + c, z)

        def got(k, i):
            part = ref.at[rows(k), block(i)]
            return copy(part, part, sem_q.at[2 * no, k, i], sem_q.at[2 * no + 1, k, i], 2 * i + c, z)

        return out, got

    a_out, a_got = share_pair(2, act)
    e_out, e_got = share_pair(3, dga)
    u_out, u_got = share_pair(4, dua)
    pw = [
        copy(wg_h.at[:, other_half], pwg, sem_pw.at[0, 0], sem_pw.at[1, 0], pm, z),
        copy(wu_h.at[:, other_half], pwu, sem_pw.at[0, 1], sem_pw.at[1, 1], pm, z),
        copy(wd_h.at[other_half], pwd, sem_pw.at[0, 2], sem_pw.at[1, 2], pm, z),
    ]

    def loop(lo, hi, body):
        def step(i, carry):
            body(i)
            return carry

        lax.fori_loop(lo, hi, step, 0)

    def partner(at, d, size):
        if size & (size - 1):
            return lax.rem(at + d, size)
        other, step = at, 1
        while step < size:
            if d & step:
                other = other + step - 2 * step * lax.rem(at // step, 2)
            step *= 2
        return other

    def dp_others(body):
        for d in range(1, n):
            body(partner(m, d, n))

    def ex_others(body):
        loop(1, e_n, lambda d: body(lax.rem(z + d, e_n)))

    def q_others(body):
        for d in range(1, q_n):
            body(partner(q, d, q_n))

    def chunks(body):
        loop(0, e_n, lambda d: body(d, lax.rem(z + e_n - d, e_n)))

    def far_first(body):
        loop(1, e_n + 1, lambda d: body(d, lax.rem(z + 2 * e_n - d, e_n)))

    def ahead(first, then):
        def step(d):
            @pl.when(d <= e_n)
            def _():
                first(lax.rem(z + 2 * e_n - d, e_n))

            @pl.when(d > 1)
            def _():
                then(d - 1, lax.rem(z + 2 * e_n - (d - 1), e_n))

        loop(1, e_n + 2, step)

    own = [
        pltpu.make_async_copy(src, dst, sem_own.at[i])
        for i, (src, dst) in enumerate(((wg_h, wg), (wu_h, wu), (wd_h, wd)))
    ]
    for one in own:
        one.start()
    barrier = pltpu.get_barrier_semaphore()
    dp_others(lambda i: pl.semaphore_signal(
        barrier, inc=1, device_id=(i, z), device_id_type=pl.DeviceIdType.MESH))
    ex_others(lambda i: pl.semaphore_signal(
        barrier, inc=1, device_id=(m, i), device_id_type=pl.DeviceIdType.MESH))
    pl.semaphore_wait(barrier, n - 1 + e_n - 1)

    dp_others(lambda i: tg_out(i).start())
    dp_others(lambda i: xa_out(i).start())
    for one in pw:
        one.start()
    wide = tok.shape[1] // 8
    for i in range(8):
        at = slice(i * wide, (i + 1) * wide)
        dys[:, at] = (cot[:, at].astype(F32) * wt[...]).astype(BF)
    dp_others(lambda i: da_out(i).start())
    tga[m] = tgt[...]
    xa[toks(m), :] = tok[:, cols(m)]
    da[toks(m), :] = dys[:, cols(m)]
    dp_others(lambda i: tg_got(i).wait_recv())
    for i in range(n):
        names = tga[i][0:1, :]
        place = lax.broadcasted_iota(jnp.int32, (e_n * slots, t_rows), 0)
        table[:, i * t_rows:(i + 1) * t_rows] = jnp.where(place == names, 1.0, 0.0).astype(BF)

    def slot_out(src, buf, own, out):
        def one(d):
            e = lax.rem(z + d, e_n)
            buf[rows(e), :] = nn(table[rows(e), :], src[...]).astype(BF)
            out(e).start()

        loop(1, e_n, one)
        own[rows(z), :] = nn(table[rows(z), :], src[...]).astype(BF)

    dp_others(lambda i: xa_got(i).wait_recv())
    slot_out(xa, xs, xr, xe_out)
    dp_others(lambda i: da_got(i).wait_recv())
    slot_out(da, ds_, dr, de_out)
    for one in own:
        one.wait()
    for one in pw:
        one.wait_recv()

    def gate_up(d, k):
        @pl.when(d > 0)
        def _():
            xe_got(k).wait_recv()

        xf(k).start()
        xf(k).wait_recv()
        for at, own_w, other_w in ((0, wg, pwg), (1, wu, pwu)):
            part = nn(xr[rows(k), :], own_w[:, my_half]) + nn(xp[rows(k), :], other_w[...])
            part = part.astype(BF)
            for i in range(q_n):
                gs[k, i, :, at * b:(at + 1) * b] = part[:, i * b:(i + 1) * b]
        q_others(lambda i: g_out(k, i).start())

    chunks(gate_up)

    def activate(d, k):
        total = gs[k, q].astype(F32)
        for dd in range(1, q_n):
            i = partner(q, dd, q_n)
            g_got(k, i).wait_recv()
            total = total + gr[k, i].astype(F32)
        gate, up = total[:, :b], total[:, b:]
        pre[rows(k), :] = gate
        upv[rows(k), :] = up
        act[rows(k), block(q)] = (gate * jax.nn.sigmoid(gate) * up).astype(BF)
        q_others(lambda i: a_out(k, i).start())

    far_first(activate)

    def down(d, k):
        @pl.when(d > 0)
        def _():
            de_got(k).wait_recv()

        df(k).start()
        df(k).wait_recv()
        part = nt(dr[rows(k), :], wd[my_half, :]) + nt(dp[rows(k), :], pwd[...])
        part = part.astype(BF)
        for i in range(q_n):
            hs[k, i] = part[:, i * b:(i + 1) * b]
        q_others(lambda i: h_out(k, i).start())

    chunks(down)

    def act_pass(k):
        q_others(lambda i: a_got(k, i).wait_recv())
        af_out(k).start()

    def result_rows(d, k):
        af_got(k).wait_recv()
        result = nn(act[rows(k), :], wd[...]).astype(BF)

        @pl.when(d == e_n)
        def _():
            rr[rows(k), :] = result

        @pl.when(d < e_n)
        def _():
            rs[rows(k), :] = result
            rb_out(k).start()

    ahead(act_pass, result_rows)

    def act_grad(d, k):
        total = hs[k, q].astype(F32)
        for dd in range(1, q_n):
            i = partner(q, dd, q_n)
            h_got(k, i).wait_recv()
            total = total + hr[k, i].astype(F32)
        gate, up = pre[rows(k), :], upv[rows(k), :]
        sig = jax.nn.sigmoid(gate)
        dga[rows(k), block(q)] = (total * up * sig * (1.0 + gate * (1.0 - sig))).astype(BF)
        dua[rows(k), block(q)] = (total * gate * sig).astype(BF)
        q_others(lambda i: e_out(k, i).start())
        q_others(lambda i: u_out(k, i).start())

    far_first(act_grad)

    def handed(k):
        q_others(lambda i: e_got(k, i).wait_recv())
        ef_out(k).start()
        q_others(lambda i: u_got(k, i).wait_recv())
        uf_out(k).start()

    def input_grad(d, k):
        ef_got(k).wait_recv()
        uf_got(k).wait_recv()
        value = (nt(dga[rows(k), :], wg[...]) + nt(dua[rows(k), :], wu[...])).astype(BF)

        @pl.when(d == e_n)
        def _():
            sr[rows(k), :] = value

        @pl.when(d < e_n)
        def _():
            ss[rows(k), :] = value
            sb_out(k).start()

    ahead(handed, input_grad)

    x_t[...] = xr[...].T
    tile = 2 * b

    def down_grad(j):
        at = pl.ds(pl.multiple_of(j * tile, 128), tile)
        gd_o[at, :] = tn(act[:, at], dr[...]).astype(BF)

    loop(0, ff // tile, down_grad)

    def give_back(src, buf, out):
        def one(d):
            i = partner(m, d, n)
            buf[toks(i), :] = tn(table[:, toks(i)], src[...]).astype(BF)
            out(i).start()

        for d in range(1, n):
            one(d)
        buf[toks(m), :] = tn(table[:, toks(m)], src[...]).astype(BF)

    ex_others(lambda i: rb_got(i).wait_recv())
    give_back(rr, un, re_out)
    res_o[:, cols(m)] = un[toks(m), :]

    def weight_grad(j):
        at = pl.ds(pl.multiple_of(j * tile, 128), tile)
        gg_o[:, at] = nn(x_t[...], dga[:, at]).astype(BF)
        gu_o[:, at] = nn(x_t[...], dua[:, at]).astype(BF)

    loop(0, ff // tile, weight_grad)
    ex_others(lambda i: sb_got(i).wait_recv())
    give_back(sr, un2, ig_out)
    ig_o[:, cols(m)] = un2[toks(m), :]

    def dp_end(i):
        re_got(i).wait_recv()
        ig_got(i).wait_recv()
        for out in (tg_out, xa_out, da_out, re_out, ig_out):
            out(i).wait_send()

    dp_others(dp_end)

    def ex_end(i):
        for out in (xe_out, de_out, rb_out, sb_out):
            out(i).wait_send()

    ex_others(ex_end)
    for one in pw:
        one.wait_send()

    def chunk_end(k):
        for out in (xf, df, af_out, ef_out, uf_out):
            out(k).wait_send()
        for out in (g_out, h_out, a_out, e_out, u_out):
            q_others(lambda i: out(k, i).wait_send())

    loop(0, e_n, chunk_end)


def fused_layer(tokens, probs, routes, w_gate, w_up, w_down, cotangent, n, e_n, cap):
    t_rows, width = tokens.shape
    w = width // n
    ff = w_gate.shape[2]
    slots, fh, q_n = n * cap, ff // 2, n // 2
    b = fh // q_n
    r = e_n * slots
    weight = probs.astype(F32)
    flat = routes.reshape(-1)
    hits = (flat[:, None] == jnp.arange(e_n, dtype=jnp.int32)[None, :]).astype(jnp.int32)
    before = jnp.cumsum(hits, axis=0) - hits
    place = jnp.sum(before * hits, axis=1)
    target = flat * slots + lax.axis_index("dp").astype(jnp.int32) * cap + place
    tgt = jnp.broadcast_to(target[None, :], (8, t_rows))
    vm = pl.BlockSpec(memory_space=pltpu.VMEM)

    def v(*shape, dtype=BF):
        return pltpu.VMEM(shape, dtype)

    scratch = [
        v(n, 8, t_rows, dtype=jnp.int32), v(r, n * t_rows),
        v(n * t_rows, w), v(n * t_rows, w),
        v(r, w), v(r, w), v(r, w), v(r, w), v(r, w), v(r, w),
        v(w, fh), v(w, fh), v(fh, w),
        v(e_n, q_n, slots, 2 * b), v(e_n, q_n, slots, 2 * b),
        v(e_n, q_n, slots, b), v(e_n, q_n, slots, b),
        v(r, b, dtype=F32), v(r, b, dtype=F32),
        v(r, ff), v(r, ff), v(r, ff),
        v(r, w), v(r, w), v(r, w), v(r, w),
        v(n * t_rows, w), v(n * t_rows, w), v(w, r), v(t_rows, width), v(w, ff), v(w, ff), v(ff, w),
        pltpu.SemaphoreType.DMA((3,)),
        pltpu.SemaphoreType.DMA((10, n)),
        pltpu.SemaphoreType.DMA((2, 3)),
        pltpu.SemaphoreType.DMA((18, e_n)),
        pltpu.SemaphoreType.DMA((10, e_n, q_n)),
    ]
    result, input_grad, gg, gu, gd = pl.pallas_call(
        functools.partial(layer_kernel, n, e_n, cap),
        out_shape=(
            jax.ShapeDtypeStruct((t_rows, width), BF),
            jax.ShapeDtypeStruct((t_rows, width), BF),
            jax.ShapeDtypeStruct((w, ff), BF),
            jax.ShapeDtypeStruct((w, ff), BF),
            jax.ShapeDtypeStruct((ff, w), BF),
        ),
        in_specs=[vm] * 4 + [pl.BlockSpec(memory_space=pl.ANY)] * 3,
        out_specs=(vm,) * 5,
        scratch_shapes=scratch,
        compiler_params=pltpu.CompilerParams(
            collective_id=0, has_side_effects=True, vmem_limit_bytes=62 * 1024 * 1024
        ),
    )(tokens, cotangent, tgt, weight, w_gate[0], w_up[0], w_down[0])
    mixed = (result.astype(F32) * weight).astype(BF)
    return mixed, input_grad, gg[None], gu[None], gd[None]


def slot_table(routes, experts_all, capacity):
    flat = routes.reshape(-1)
    hits = (flat[:, None] == jnp.arange(experts_all, dtype=jnp.int32)[None, :]).astype(jnp.int32)
    before = jnp.cumsum(hits, axis=0) - hits
    place = jnp.sum(before * hits, axis=1)
    target = flat * capacity + place
    table = jnp.arange(experts_all * capacity, dtype=jnp.int32)[:, None] == target[None, :]
    return table.astype(jnp.bfloat16)


def spread_rows(table, values, slices):
    shaped = values.reshape(values.shape[0], slices, values.shape[1] // slices)
    return jnp.einsum("st,tnk->nsk", table, shaped, preferred_element_type=jnp.float32).astype(
        jnp.bfloat16
    )


def to_rows(received, local_count):
    sources, slots, width = received.shape
    shaped = received.reshape(sources, local_count, slots // local_count, width)
    shaped = jnp.swapaxes(shaped, 1, 2)
    return shaped.reshape(sources * (slots // local_count), local_count, width)


def to_sources(rowwise, capacity):
    total, local_count, width = rowwise.shape
    shaped = rowwise.reshape(total // capacity, capacity, local_count, width)
    shaped = jnp.swapaxes(shaped, 1, 2)
    return shaped.reshape(total // capacity, local_count * capacity, width)


def collect(table, back, tok_rows, top):
    picked = jnp.einsum("st,nsk->tnk", table, back, preferred_element_type=jnp.float32)
    return picked.reshape(tok_rows, top, -1)


def per_device(tokens, probs, routes, w_gate, w_up, w_down, cotangent):
    local_count = w_gate.shape[0]
    n_dp = lax.axis_size("dp")
    n_exp = lax.axis_size("expert")
    experts_all = local_count * n_exp
    tok_rows, width = tokens.shape
    top = routes.shape[1]
    capacity = max(2, 17 * tok_rows * top // (16 * experts_all))
    ff = w_gate.shape[2]
    if (
        local_count == 1 and top == 1 and n_dp % 2 == 0 and ff % (n_dp * 128) == 0
        and tok_rows % 128 == 0 and width % (n_dp * 128) == 0 and (n_dp * capacity) % 16 == 0
    ):
        return fused_layer(
            tokens, probs, routes, w_gate, w_up, w_down, cotangent, n_dp, n_exp, capacity
        )
    blocks = n_dp * n_exp
    slot_width = width // n_dp
    table = slot_table(routes, experts_all, capacity)
    x_send = spread_rows(table, jnp.repeat(tokens, top, axis=0), n_dp)
    x_send = x_send.reshape(blocks, local_count * capacity, slot_width)
    weight = probs.astype(jnp.float32)
    scaled = (jnp.repeat(cotangent, top, axis=0).astype(jnp.float32) * weight).astype(jnp.bfloat16)
    x_got = lax.all_to_all(x_send, ("dp", "expert"), split_axis=0, concat_axis=0, tiled=True)
    rows = to_rows(x_got, local_count)
    part = rows
    gate = jnp.einsum("red,edf->ref", part, w_gate, preferred_element_type=jnp.float32)
    upper = jnp.einsum("red,edf->ref", part, w_up, preferred_element_type=jnp.float32)
    summed = lax.psum_scatter(
        jnp.stack([gate, upper], axis=2).astype(jnp.bfloat16), "dp", scatter_dimension=0, tiled=True
    ).astype(jnp.float32)
    gate_pre = summed[:, :, 0]
    up_value = summed[:, :, 1]
    sig = jax.nn.sigmoid(gate_pre)
    act = (gate_pre * sig * up_value).astype(jnp.bfloat16)
    act_all = lax.all_gather(act, "dp", axis=0, tiled=True)
    result = jnp.einsum("ref,efd->red", act_all, w_down, preferred_element_type=jnp.float32).astype(
        jnp.bfloat16
    )
    outgoing = to_sources(result, capacity)
    back = lax.all_to_all(outgoing, ("dp", "expert"), split_axis=0, concat_axis=0, tiled=True)
    back = back.reshape(n_dp, experts_all * capacity, slot_width)
    picked = collect(table, back, tok_rows, top)
    mixed = jnp.sum(picked * weight[..., None], axis=1).astype(jnp.bfloat16)
    dy_send = spread_rows(table, scaled, n_dp).reshape(blocks, local_count * capacity, slot_width)
    dy_got = lax.all_to_all(dy_send, ("dp", "expert"), split_axis=0, concat_axis=0, tiled=True)
    dout = to_rows(dy_got, local_count)
    grad_down = jnp.einsum("ref,red->efd", act_all, dout, preferred_element_type=jnp.float32)
    part = dout
    dact = lax.psum_scatter(
        jnp.einsum("red,efd->ref", part, w_down, preferred_element_type=jnp.float32).astype(
            jnp.bfloat16
        ),
        "dp",
        scatter_dimension=0,
        tiled=True,
    ).astype(jnp.float32)
    dgate = (dact * up_value * sig * (1.0 + gate_pre * (1.0 - sig))).astype(jnp.bfloat16)
    dup = (dact * gate_pre * sig).astype(jnp.bfloat16)
    dgate_all, dup_all = (
        lax.all_gather(dgate, "dp", axis=0, tiled=True),
        lax.all_gather(dup, "dp", axis=0, tiled=True),
    )
    grad_gate = jnp.einsum("red,ref->edf", rows, dgate_all, preferred_element_type=jnp.float32)
    grad_up = jnp.einsum("red,ref->edf", rows, dup_all, preferred_element_type=jnp.float32)
    slot_grad = jnp.einsum(
        "ref,edf->red", dgate_all, w_gate, preferred_element_type=jnp.float32
    ) + jnp.einsum("ref,edf->red", dup_all, w_up, preferred_element_type=jnp.float32)
    slot_grad = slot_grad.astype(jnp.bfloat16)
    returned = lax.all_to_all(
        to_sources(slot_grad, capacity), ("dp", "expert"), split_axis=0, concat_axis=0, tiled=True
    )
    returned = returned.reshape(n_dp, experts_all * capacity, slot_width)
    input_grad = jnp.sum(collect(table, returned, tok_rows, top), axis=1).astype(jnp.bfloat16)
    return (
        mixed,
        input_grad,
        grad_gate.astype(jnp.bfloat16),
        grad_up.astype(jnp.bfloat16),
        grad_down.astype(jnp.bfloat16),
    )


def solution(mesh):
    return jax.shard_map(
        per_device,
        mesh=mesh,
        in_specs=(
            P(("dp", "expert"), None),
            P(("dp", "expert"), None),
            P(("dp", "expert"), None),
            P("expert", "dp", None),
            P("expert", "dp", None),
            P("expert", None, "dp"),
            P(("dp", "expert"), None),
        ),
        out_specs=(
            P(("dp", "expert"), None),
            P(("dp", "expert"), None),
            P("expert", "dp", None),
            P("expert", "dp", None),
            P("expert", None, "dp"),
        ),
        check_vma=False,
    )
```
